32 devices in a mesh: pb: 8 (over z, x), ta: 4 (over y, core).
Axes of the slice: x: 2, y: 2, z: 4, core: 2. Of those that a mesh axis runs over, the one named last changes fastest.
Arguments:
- feat_one: bfloat16 [16, 256, 128], P('pb'), may hold values from -7 to 7
- feat_two: bfloat16 [4, 2048, 128], P('ta', 'pb'), may hold values from -7 to 7
- cot_flow: float32 [2, 16, 256], P(None, 'pb'), may hold values from -6 to 6
- enc_input: bfloat16 [16, 128, 256], P('pb', 'ta'), may hold values from -0.59765625 to 0.59765625
- enc_weight: bfloat16 [3, 3, 128, 128], P(None, None, 'ta'), may hold values from -0.1875 to 0.1875
Outputs:
- grad_two: float32 [4, 2048, 128], P('ta', 'pb')
- grad_input: float32 [16, 128, 256], P('pb', 'ta')
- grad_weight: float32 [3, 3, 128, 128], P(None, None, 'ta')
The draws below stay inside these ranges and needn't reach their ends.
All inputs are finite; a program needn't handle non-finite values.
Results may differ from the reference program's by a relative error of at most 0.0047.
Values may be sent and summed in bfloat16 or wider, within the bound.
A program may use at most 64 MiB of HBM per device.

```python
import math
import jax
import jax.numpy as jnp
from jax import lax

C = 128
CIN = 128
QCOLS = 256
FRAME_COLS = 512
QROWS = 16
QUERIES = 4096
GROUP_TGT = 2048
TARGETS = 8192
N_TA = 4


def feature_pair(key):
    key_one = jax.random.fold_in(key, 11)
    key_two = jax.random.fold_in(key, 12)
    base_one = 1.5 * jax.random.truncated_normal(key_one, -4.0, 4.0, (QUERIES, C), jnp.float32)
    base_two = 1.5 * jax.random.truncated_normal(key_two, -4.0, 4.0, (TARGETS, C), jnp.float32)
    return (base_one, base_two)


def draw_feat_one(key, part):
    return feature_pair(key)[0].reshape(QROWS, QCOLS, C).astype(jnp.bfloat16)


def draw_feat_two(key, part):
    return feature_pair(key)[1].reshape(N_TA, GROUP_TGT, C).astype(jnp.bfloat16)


def steps_of(key, shape, split, least, top_value):
    loudness, own = 1.0, jax.random.fold_in(key, 6)
    for dim, blocks in split:
        heights = jnp.exp(jax.random.uniform(jax.random.fold_in(own, dim), (blocks,), jnp.float32, least / len(split), top_value / len(split)))
        loudness = loudness * jnp.repeat(heights, shape[dim] // blocks).reshape([-1 if axis == dim else 1 for axis in range(len(shape))])
    return loudness


def centred(rng, shape, scale, reach, pieces=(), kind=jnp.bfloat16):
    array = scale * jax.random.normal(rng, shape, jnp.float32)
    if pieces:
        array = array * steps_of(rng, shape, pieces, -0.22, 0.18)
    return jnp.clip(array, -reach, reach).astype(kind)


def setup_inputs(seed: int = 0) -> dict:
    key_list = jax.random.split(jax.random.key(seed), 6)
    feat_one = draw_feat_one(jax.random.fold_in(key_list[5], 71), 0)
    feat_two = draw_feat_two(jax.random.fold_in(key_list[5], 71), 0)
    cot_flow = centred(key_list[2], (2, QROWS, QCOLS), 1.0, 6.0, ((1, 8),), jnp.float32)
    enc_input = centred(key_list[3], (QROWS, CIN, QCOLS), 0.1, 0.59765625, ((0, 8), (1, 4)))
    enc_weight = centred(key_list[4], (3, 3, CIN, C), (9 * CIN) ** -0.5, 0.1875, ((2, 4),))
    return dict(feat_one=feat_one, feat_two=feat_two, cot_flow=cot_flow, enc_input=enc_input, enc_weight=enc_weight)


def target_positions():
    index_all = jnp.arange(TARGETS, dtype=jnp.int32)
    col_pos = (index_all % FRAME_COLS).astype(jnp.float32) - FRAME_COLS / 2
    row_pos = (index_all // FRAME_COLS).astype(jnp.float32)
    return (col_pos, row_pos)

def reference(feat_one, feat_two, cot_flow, enc_input, enc_weight):
    inv_scale = 1.0 / math.sqrt(C)
    queries = feat_one.reshape(QUERIES, C)
    queries_wide = queries.astype(jnp.float32)
    targets = feat_two.reshape(TARGETS, C)
    targets_wide = targets.astype(jnp.float32)
    flow_rows = cot_flow.reshape(2, QUERIES)
    col_pos, row_pos = target_positions()
    block_rows = 512 if QUERIES % 512 == 0 else QUERIES
    nblocks = QUERIES // block_rows

    def step_block(accum, block_index):
        offset = (block_index * block_rows).astype(jnp.int32)
        rows = lax.dynamic_slice_in_dim(queries_wide, offset, block_rows, 0)
        flows = lax.dynamic_slice_in_dim(flow_rows, offset, block_rows, 1)
        scores = jnp.dot(rows, targets_wide.T, preferred_element_type=jnp.float32) * inv_scale
        peak = lax.optimization_barrier(jnp.max(scores, axis=1, keepdims=True))
        expo = jnp.exp(scores - peak)
        prob = expo / lax.optimization_barrier(jnp.sum(expo, axis=1, keepdims=True))
        pull = flows[0][:, None] * col_pos[None, :] + flows[1][:, None] * row_pos[None, :]
        mean_pull = lax.optimization_barrier(jnp.sum(prob * pull, axis=1, keepdims=True))
        score_grad = (prob * (pull - mean_pull) * inv_scale).astype(jnp.bfloat16)
        grad_wide = score_grad.astype(jnp.float32)
        feat_part = jnp.dot(grad_wide, targets_wide, preferred_element_type=jnp.float32).astype(jnp.bfloat16)
        accum = accum + jnp.dot(grad_wide.T, rows, preferred_element_type=jnp.float32)
        return (accum, feat_part)
    accum, feat_parts = lax.scan(step_block, jnp.zeros((TARGETS, C), jnp.float32), jnp.arange(nblocks, dtype=jnp.int32))
    grad_two = accum.reshape(N_TA, GROUP_TGT, C)
    feat_grad = feat_parts.reshape(QROWS, QCOLS, C)
    padded = jnp.pad(feat_grad, ((1, 1), (1, 1), (0, 0))).astype(jnp.float32)
    input_wide = enc_input.astype(jnp.float32)
    weight_wide = enc_weight.astype(jnp.float32)
    grad_input = jnp.zeros((QROWS, CIN, QCOLS), jnp.float32)
    weight_parts = []
    for row_off in range(3):
        for col_off in range(3):
            shifted = padded[2 - row_off:2 - row_off + QROWS, 2 - col_off:2 - col_off + QCOLS]
            grad_input = grad_input + jnp.einsum('yxo,io->yix', shifted, weight_wide[row_off, col_off])
            weight_parts.append(jnp.einsum('yix,yxo->io', input_wide, shifted))
    grad_weight = jnp.stack(weight_parts).reshape(3, 3, CIN, C)
    return (grad_two, grad_input, grad_weight)
```

```python
import functools
import math

import jax
import jax.numpy as jnp
from jax import lax
from jax.experimental import pallas as pl
from jax.experimental.pallas import tpu as pltpu
from jax.sharding import PartitionSpec as P

FRAME_COLS = 512
MESH = pl.DeviceIdType.MESH
F32 = jnp.float32
BF16 = jnp.bfloat16


def remote(src, dst, send_sem, recv_sem, where):
    return pltpu.make_async_remote_copy(
        src_ref=src,
        dst_ref=dst,
        send_sem=send_sem,
        recv_sem=recv_sem,
        device_id=where,
        device_id_type=MESH,
    )


def matmul(left, right, dims):
    return lax.dot_general(left, right, (dims, ((), ())), preferred_element_type=F32)


def moved(value, step):
    if step == 0:
        return value
    width = value.shape[1]
    lane = lax.broadcasted_iota(jnp.int32, value.shape, 1)
    rolled = pltpu.roll(value, step % width, 1)
    edge = 0 if step > 0 else width - 1
    return jnp.where(lane == edge, 0.0, rolled)


def kernel(
    n_pb, n_ta, rows, cols, gw_rows,
    q_ref, k_ref, flow_ref, in_ref, w_ref,
    g2_ref, gi_ref, gw_ref,
    k_all, expo, iota, peaks, totals, pulls, stats, stats_in,
    g_out, g_in, f_part, f_in, f_all, halo_in, in_sh, z_buf,
    edge_out, edge_in, gw_part, gw_send, gw_in, gw_all,
    kz_send, kx_send, k_recv, s_send, s_recv, g_send, g_recv,
    f_send, f_recv, a_send, a_recv, h_send, h_recv, e_send, e_recv,
    w_send, w_recv, v_send, v_recv,
):
    me = lax.axis_index("pb")
    grp = lax.axis_index("ta")
    zz, xx = me // 2, me % 2
    n_z = n_pb // 2
    mate = zz * 2 + (1 - xx)
    n_q, chan = q_ref.shape
    tgt = k_ref.shape[0]
    n_own = gw_part.shape[0] // gw_rows
    inv_scale = 1.0 / math.sqrt(chan)
    unit = inv_scale / math.log(2.0)

    barrier = pltpu.get_barrier_semaphore()

    def greet(d, _):
        pl.semaphore_signal(
            barrier, inc=1, device_id={"pb": lax.rem(me + d, n_pb)}, device_id_type=MESH
        )
        return 0

    lax.fori_loop(1, n_pb, greet, 0)
    for d in range(1, n_ta):
        pl.semaphore_signal(
            barrier, inc=1, device_id={"ta": lax.rem(grp + d, n_ta)}, device_id_type=MESH
        )
    k_all[me] = k_ref[...]
    iota[...] = lax.broadcasted_iota(jnp.int32, (tgt, n_q), 0).astype(F32)
    pl.semaphore_wait(barrier, n_pb - 1 + n_ta - 1)

    def z_copy(d):
        to = lax.rem(zz + d, n_z)
        return remote(
            k_ref, k_all.at[me], kz_send.at[d], k_recv.at[me], {"pb": to * 2 + xx}
        )

    def x_copy(d):
        origin = lax.rem(zz + n_z - d, n_z) * 2 + xx
        return remote(
            k_all.at[origin], k_all.at[origin], kx_send.at[d], k_recv.at[origin], {"pb": mate}
        )

    own_copy = remote(k_ref, k_all.at[me], kx_send.at[0], k_recv.at[me], {"pb": mate})
    own_copy.start()
    for d in range(1, n_z):
        z_copy(d).start()

    up = {"pb": lax.rem(me + 1, n_pb)}
    down = {"pb": lax.rem(me + n_pb - 1, n_pb)}
    h_up = remote(in_ref.at[rows - 1], halo_in.at[0], h_send.at[0], h_recv.at[0], up)
    h_down = remote(in_ref.at[0], halo_in.at[1], h_send.at[1], h_recv.at[1], down)
    h_up.start()
    h_down.start()

    def score_block(origin):
        raw = matmul(k_all[origin], q_ref[...], ((1,), (1,)))
        peak = jnp.max(raw, axis=0, keepdims=True) * unit
        value = jnp.exp2(raw * unit - peak)
        expo[origin] = value
        k0 = (grp * n_pb + origin) * tgt
        col0 = (lax.rem(k0, FRAME_COLS) - FRAME_COLS // 2).astype(F32)
        row = (k0 // FRAME_COLS).astype(F32)
        total = jnp.sum(value, axis=0, keepdims=True)
        along = jnp.sum(value * iota[...], axis=0, keepdims=True)
        peaks[origin] = peak
        totals[origin] = total
        pulls[origin] = flow_ref[0:1, :] * (along + col0 * total) + flow_ref[1:2, :] * (
            row * total
        )

    score_block(me)
    for y in range(rows):
        value = in_ref[y].astype(F32)
        cin = value.shape[0]
        for b in range(3):
            in_sh[b * cin : (b + 1) * cin, (y + 1) * cols : (y + 2) * cols] = moved(
                value, 1 - b
            ).astype(BF16)

    def arrived(origin):
        remote(
            k_all.at[origin], k_all.at[origin], kx_send.at[0], k_recv.at[origin], {"pb": mate}
        ).wait_recv()

    arrived(mate)
    score_block(mate)

    def z_step(d, _):
        origin = lax.rem(zz + n_z - d, n_z) * 2 + xx
        arrived(origin)
        x_copy(d).start()
        score_block(origin)
        return 0

    lax.fori_loop(1, n_z, z_step, 0)

    def x_step(d, _):
        origin = lax.rem(zz + n_z - d, n_z) * 2 + (1 - xx)
        arrived(origin)
        score_block(origin)
        return 0

    lax.fori_loop(1, n_z, x_step, 0)

    all_peaks = peaks[...]
    peak = jnp.max(all_peaks, axis=0)
    decay = jnp.exp2(all_peaks - peak[None])
    stats[0:1, :] = peak
    stats[1:2, :] = jnp.sum(totals[...] * decay, axis=0)
    stats[2:3, :] = jnp.sum(pulls[...] * decay, axis=0)
    stat_copies = []
    for d in range(1, n_ta):
        stat_copies.append(
            remote(
                stats,
                stats_in.at[grp],
                s_send.at[d],
                s_recv.at[grp],
                {"ta": lax.rem(grp + d, n_ta)},
            )
        )
        stat_copies[-1].start()

    h_up.wait_recv()
    h_down.wait_recv()
    for side, place in ((0, 0), (1, rows + 1)):
        value = halo_in[side].astype(F32)
        at_end = (me == 0) if side == 0 else (me == n_pb - 1)
        value = value * jnp.where(at_end, 0.0, 1.0)
        for b in range(3):
            in_sh[b * cin : (b + 1) * cin, place * cols : (place + 1) * cols] = moved(
                value, 1 - b
            ).astype(BF16)

    run = (stats[0:1, :], stats[1:2, :], stats[2:3, :])
    for d in range(1, n_ta):
        frm = lax.rem(grp + n_ta - d, n_ta)
        remote(
            stats, stats_in.at[frm], s_send.at[d], s_recv.at[frm], {"ta": frm}
        ).wait_recv()
        other = stats_in[frm]
        top = jnp.maximum(run[0], other[0:1, :])
        one = jnp.exp2(run[0] - top)
        two = jnp.exp2(other[0:1, :] - top)
        run = (
            top,
            run[1] * one + other[1:2, :] * two,
            run[2] * one + other[2:3, :] * two,
        )
    peak, total, weighted = run
    mean = weighted / total
    weight = inv_scale / total
    stats_in[grp, 0:1, :] = peak
    stats_in[grp, 1:2, :] = mean
    stats_in[grp, 2:3, :] = weight
    f_part[...] = jnp.zeros_like(f_part)

    def grad_block(origin):
        k0 = (grp * n_pb + origin) * tgt
        col0 = (lax.rem(k0, FRAME_COLS) - FRAME_COLS // 2).astype(F32)
        row = (k0 // FRAME_COLS).astype(F32)
        scale = jnp.exp2(peaks[origin] - stats_in[grp, 0:1, :]) * stats_in[grp, 2:3, :]
        slope = flow_ref[0:1, :]
        rest = col0 * slope + row * flow_ref[1:2, :] - stats_in[grp, 1:2, :]
        grad = (expo[origin] * scale * (iota[...] * slope + rest)).astype(BF16)
        f_part[...] += matmul(k_all[origin], grad, ((0,), (0,)))
        return matmul(grad, q_ref[...], ((1,), (0,)))

    def g_copy(d):
        to = lax.rem(me + d, n_pb)
        return remote(g_out.at[to], g_in.at[me], g_send.at[d], g_recv.at[me], {"pb": to})

    def grad_step(d, _):
        to = lax.rem(me + d, n_pb)
        g_out[to] = grad_block(to).astype(BF16)
        g_copy(d).start()
        return 0

    lax.fori_loop(1, n_pb, grad_step, 0)
    g2_ref[...] = grad_block(me)

    part = chan // n_ta

    def rows_of(ref, index):
        return ref.at[pl.ds(pl.multiple_of(index * part, part), part), :]

    f_all[...] = f_part[...].astype(BF16)
    f_copies = []
    for d in range(1, n_ta):
        to = lax.rem(grp + d, n_ta)
        f_copies.append(
            remote(rows_of(f_all, to), f_in.at[grp], f_send.at[d], f_recv.at[grp], {"ta": to})
        )
        f_copies[-1].start()
    total_f = f_part[pl.ds(pl.multiple_of(grp * part, part), part), :]
    for d in range(1, n_ta):
        frm = lax.rem(grp + n_ta - d, n_ta)
        remote(
            f_in.at[frm], f_in.at[frm], f_send.at[d], f_recv.at[frm], {"ta": frm}
        ).wait_recv()
        total_f = total_f + f_in[frm].astype(F32)
    for copy in f_copies:
        copy.wait_send()
    z_buf[pl.ds(pl.multiple_of(grp * part, part), part), :] = total_f.astype(BF16)
    a_copies = []
    for d in range(1, n_ta):
        to = lax.rem(grp + d, n_ta)
        a_copies.append(
            remote(
                rows_of(z_buf, grp), rows_of(z_buf, grp), a_send.at[d], a_recv.at[grp], {"ta": to}
            )
        )
        a_copies[-1].start()
    for d in range(1, n_ta):
        frm = lax.rem(grp + n_ta - d, n_ta)
        remote(
            rows_of(z_buf, frm), rows_of(z_buf, frm), a_send.at[d], a_recv.at[frm], {"ta": frm}
        ).wait_recv()

    feat = z_buf[...]
    width = 3 * cin
    for a in range(3):
        gw_part[a * width : (a + 1) * width, :] = matmul(
            in_sh[:, a * cols : (a + rows) * cols], feat, ((1,), (1,))
        )
    gw_send[...] = gw_part[...].astype(BF16)

    def gw_chunk(ref, index):
        return ref.at[pl.ds(pl.multiple_of(index * gw_rows, gw_rows), gw_rows), :]

    def w_copy(d):
        to = lax.rem(me + d, n_pb)
        return to, remote(
            gw_chunk(gw_send, to), gw_in.at[me], w_send.at[d], w_recv.at[me], {"pb": to}
        )

    def w_start(d, _):
        to = lax.rem(me + d, n_pb)

        @pl.when(to < n_own)
        def _():
            w_copy(d)[1].start()

        return 0

    lax.fori_loop(1, n_pb, w_start, 0)

    spread = matmul(w_ref[...], feat, ((1,), (0,)))
    outs = [None] * (rows + 2)
    for r in range(rows):
        for a in range(3):
            term = None
            for b in range(3):
                first = (a * 3 + b) * cin
                piece = moved(
                    spread[first : first + cin, r * cols : (r + 1) * cols], b - 1
                )
                term = piece if term is None else term + piece
            place = r + a
            outs[place] = term if outs[place] is None else outs[place] + term
    edge_out[0] = outs[rows + 1]
    edge_out[1] = outs[0]
    e_up = remote(edge_out.at[0], edge_in.at[0], e_send.at[0], e_recv.at[0], up)
    e_down = remote(edge_out.at[1], edge_in.at[1], e_send.at[1], e_recv.at[1], down)
    e_up.start()
    e_down.start()
    for y in range(rows):
        gi_ref[y] = outs[y + 1]

    @pl.when(me < n_own)
    def _():
        first = pl.multiple_of(me * gw_rows, gw_rows)
        gw_all[pl.ds(first, gw_rows), :] = gw_part[pl.ds(first, gw_rows), :]

        def add(d, _):
            frm = lax.rem(me + n_pb - d, n_pb)
            remote(
                gw_in.at[frm], gw_in.at[frm], w_send.at[d], w_recv.at[frm], {"pb": frm}
            ).wait_recv()
            gw_all[pl.ds(first, gw_rows), :] += gw_in[frm].astype(F32)
            return 0

        lax.fori_loop(1, n_pb, add, 0)

        def give(d, _):
            to = lax.rem(me + d, n_pb)
            remote(
                gw_chunk(gw_all, me), gw_chunk(gw_all, me), v_send.at[d], v_recv.at[me],
                {"pb": to},
            ).start()
            return 0

        lax.fori_loop(1, n_pb, give, 0)

    def g_add(d, _):
        frm = lax.rem(me + n_pb - d, n_pb)
        remote(
            g_in.at[frm], g_in.at[frm], g_send.at[d], g_recv.at[frm], {"pb": frm}
        ).wait_recv()
        g2_ref[...] += g_in[frm].astype(F32)
        return 0

    lax.fori_loop(1, n_pb, g_add, 0)

    e_up.wait_recv()
    e_down.wait_recv()
    gi_ref[0] += edge_in[0] * jnp.where(me == 0, 0.0, 1.0)
    gi_ref[rows - 1] += edge_in[1] * jnp.where(me == n_pb - 1, 0.0, 1.0)

    def v_wait(d, _):
        frm = lax.rem(me + n_pb - d, n_pb)

        @pl.when(frm < n_own)
        def _():
            remote(
                gw_chunk(gw_all, frm), gw_chunk(gw_all, frm), v_send.at[d], v_recv.at[frm],
                {"pb": frm},
            ).wait_recv()

        return 0

    lax.fori_loop(1, n_pb, v_wait, 0)
    gw_ref[...] = gw_all[...]

    own_copy.wait_send()
    for d in range(1, n_z):
        z_copy(d).wait_send()
        x_copy(d).wait_send()
    for copy in (h_up, h_down, e_up, e_down, *stat_copies, *a_copies):
        copy.wait_send()

    def drain(d, _):
        g_copy(d).wait_send()

        @pl.when(lax.rem(me + d, n_pb) < n_own)
        def _():
            w_copy(d)[1].wait_send()

        @pl.when(me < n_own)
        def _():
            remote(
                gw_chunk(gw_all, me), gw_chunk(gw_all, me), v_send.at[d], v_recv.at[me],
                {"pb": lax.rem(me + d, n_pb)},
            ).wait_send()

        return 0

    lax.fori_loop(1, n_pb, drain, 0)


def per_device(n_pb, n_ta, feat_one, feat_two, cot_flow, enc_input, enc_weight):
    rows, cols, chan = feat_one.shape
    n_q = rows * cols
    tgt = feat_two.shape[1]
    cin = enc_input.shape[1]
    taps = 9 * cin
    assert n_pb % 2 == 0 and FRAME_COLS % tgt == 0 and taps % 16 == 0
    gw_rows = 16 * pl.cdiv(taps // 16, n_pb)
    assert taps % gw_rows == 0
    vmem = pl.BlockSpec(memory_space=pltpu.VMEM)
    dma = pltpu.SemaphoreType.DMA
    n_z = n_pb // 2
    outs = pl.pallas_call(
        functools.partial(kernel, n_pb, n_ta, rows, cols, gw_rows),
        out_shape=(
            jax.ShapeDtypeStruct((tgt, chan), F32),
            jax.ShapeDtypeStruct((rows, cin, cols), F32),
            jax.ShapeDtypeStruct((taps, chan), F32),
        ),
        in_specs=[vmem] * 5,
        out_specs=(vmem,) * 3,
        scratch_shapes=[
            pltpu.VMEM((n_pb, tgt, chan), BF16),
            pltpu.VMEM((n_pb, tgt, n_q), F32),
            pltpu.VMEM((tgt, n_q), F32),
            pltpu.VMEM((n_pb, 1, n_q), F32),
            pltpu.VMEM((n_pb, 1, n_q), F32),
            pltpu.VMEM((n_pb, 1, n_q), F32),
            pltpu.VMEM((8, n_q), F32),
            pltpu.VMEM((n_ta, 8, n_q), F32),
            pltpu.VMEM((n_pb, tgt, chan), BF16),
            pltpu.VMEM((n_pb, tgt, chan), BF16),
            pltpu.VMEM((chan, n_q), F32),
            pltpu.VMEM((n_ta, chan // n_ta, n_q), BF16),
            pltpu.VMEM((chan, n_q), BF16),
            pltpu.VMEM((2, cin, cols), BF16),
            pltpu.VMEM((3 * cin, (rows + 2) * cols), BF16),
            pltpu.VMEM((chan, n_q), BF16),
            pltpu.VMEM((2, cin, cols), F32),
            pltpu.VMEM((2, cin, cols), F32),
            pltpu.VMEM((taps, chan), F32),
            pltpu.VMEM((taps, chan), BF16),
            pltpu.VMEM((n_pb, gw_rows, chan), BF16),
            pltpu.VMEM((taps, chan), F32),
            dma((n_z,)), dma((n_z,)), dma((n_pb,)),
            dma((n_ta,)), dma((n_ta,)),
            dma((n_pb,)), dma((n_pb,)),
            dma((n_ta,)), dma((n_ta,)),
            dma((n_ta,)), dma((n_ta,)),
            dma((2,)), dma((2,)),
            dma((2,)), dma((2,)),
            dma((n_pb,)), dma((n_pb,)),
            dma((n_pb,)), dma((n_pb,)),
        ],
        compiler_params=pltpu.CompilerParams(collective_id=0, has_side_effects=True),
        name="matching",
    )(
        feat_one.reshape(n_q, chan),
        feat_two[0],
        cot_flow.reshape(2, n_q),
        enc_input,
        enc_weight.reshape(taps, chan),
    )
    return (
        outs[0][None],
        outs[1],
        outs[2].reshape(3, 3, cin, chan),
    )


def solution(mesh):
    in_specs = (
        P("pb", None, None),
        P("ta", "pb", None),
        P(None, "pb", None),
        P("pb", "ta", None),
        P(None, None, "ta", None),
    )
    out_specs = (P("ta", "pb", None), P("pb", "ta", None), P(None, None, "ta", None))
    body = functools.partial(per_device, mesh.shape["pb"], mesh.shape["ta"])
    return jax.shard_map(
        body, mesh=mesh, in_specs=in_specs, out_specs=out_specs, check_vma=False
    )
```

```python
import functools
import math

import jax
import jax.numpy as jnp
from jax import lax
from jax.experimental import pallas as pl
from jax.experimental.pallas import tpu as pltpu
from jax.sharding import PartitionSpec as P

FRAME_COLS = 512
MESH = pl.DeviceIdType.MESH
F32 = jnp.float32
BF16 = jnp.bfloat16


def remote(src, dst, send_sem, recv_sem, where):
    return pltpu.make_async_remote_copy(
        src_ref=src,
        dst_ref=dst,
        send_sem=send_sem,
        recv_sem=recv_sem,
        device_id=where,
        device_id_type=MESH,
    )


def matmul(left, right, dims):
    return lax.dot_general(left, right, (dims, ((), ())), preferred_element_type=F32)


def moved(value, step):
    if step == 0:
        return value
    width = value.shape[1]
    lane = lax.broadcasted_iota(jnp.int32, value.shape, 1)
    rolled = pltpu.roll(value, step % width, 1)
    edge = 0 if step > 0 else width - 1
    return jnp.where(lane == edge, 0.0, rolled)


def kernel(
    n_pb, n_ta, rows, cols, gw_rows,
    q_ref, k_ref, flow_ref, in_ref, w_ref,
    g2_ref, gi_ref, gw_ref,
    q_all, flow_in, flow_all, k_all, expo, grads, iota, peaks, totals, pulls, stats, stats_in,
    finals, g_out, g_in, f_part, f_out, f_in, feat_ref, halo_in, in_sh,
    edge_out, edge_in, gw_part, gw_send, gw_in, gw_all,
    q_send, q_recv, k_send, k_recv, s_send, s_recv, g_send, g_recv,
    f_send, f_recv, a_send, a_recv, h_send, h_recv, e_send, e_recv,
    w_send, w_recv, v_send, v_recv,
):
    me = lax.axis_index("pb")
    grp = lax.axis_index("ta")
    zz, xx = me // 2, me % 2
    n_z = n_pb // 2
    other = 1 - xx
    mate = zz * 2 + other
    n_q, chan = q_ref.shape
    tgt = k_ref.shape[0]
    n_own = gw_part.shape[0] // gw_rows
    inv_scale = 1.0 / math.sqrt(chan)
    unit = inv_scale / math.log(2.0)
    team = [(dx, dt) for dx in (1, 0) for dt in range(n_ta - 1, -1, -1) if dx or dt]

    def mate_at(dx, dt):
        x, t = lax.rem(xx + dx, 2), lax.rem(grp + dt, n_ta)
        return x, t, {"pb": zz * 2 + x, "ta": t}

    def source_at(dx, dt):
        x, t = lax.rem(xx + dx, 2), lax.rem(grp + n_ta - dt, n_ta)
        return x * n_ta + t

    slot = xx * n_ta + grp

    barrier = pltpu.get_barrier_semaphore()

    def greet(d, _):
        pl.semaphore_signal(
            barrier, inc=1, device_id={"pb": lax.rem(me + d, n_pb)}, device_id_type=MESH
        )
        return 0

    lax.fori_loop(1, n_pb, greet, 0)
    for dx, dt in team:
        if dt:
            pl.semaphore_signal(
                barrier, inc=1, device_id=mate_at(dx, dt)[2], device_id_type=MESH
            )

    def spread_flow(ref, half):
        for r in range(rows):
            for comp in range(2):
                flow_all[half, comp : comp + 1, r * cols : (r + 1) * cols] = ref[
                    comp, r : r + 1, :
                ]

    def place_of(origin):
        k0 = (grp * n_pb + origin * 2 + xx) * tgt
        col0 = (lax.rem(k0, FRAME_COLS) - FRAME_COLS // 2).astype(F32)
        return col0, (k0 // FRAME_COLS).astype(F32)

    def score_block(origin, half):
        raw = matmul(k_all[origin], q_all[half], ((1,), (1,)))
        peak = jnp.max(raw, axis=0, keepdims=True) * unit
        value = jnp.exp2(raw * unit - peak)
        index = half * n_z + origin
        expo[index] = value
        col0, row = place_of(origin)
        total = jnp.sum(value, axis=0, keepdims=True)
        along = jnp.sum(value * iota[...], axis=0, keepdims=True)
        peaks[index] = peak
        totals[index] = total
        pulls[index] = flow_all[half, 0:1, :] * (along + col0 * total) + flow_all[
            half, 1:2, :
        ] * (row * total)

    k_all[zz] = k_ref[...]
    q_all[xx] = q_ref[...]
    spread_flow(flow_ref, xx)
    iota[...] = lax.broadcasted_iota(jnp.int32, (tgt, n_q), 0).astype(F32)
    score_block(zz, xx)
    pl.semaphore_wait(barrier, n_pb - 1 + 2 * (n_ta - 1))

    q_copy = remote(q_ref, q_all.at[xx], q_send.at[0], q_recv.at[0], {"pb": mate})
    flow_copy = remote(flow_ref, flow_in, q_send.at[1], q_recv.at[1], {"pb": mate})
    q_copy.start()
    flow_copy.start()

    def near(fn):
        def step(t, _):
            dist = t // 2 + 1
            z = zz + dist * (1 - 2 * (t % 2))

            @pl.when(jnp.logical_and(z >= 0, z < n_z))
            def _():
                fn(z)

            return 0

        lax.fori_loop(0, 2 * (n_z - 1), step, 0)

    def k_copy(z):
        return remote(
            k_ref, k_all.at[zz], k_send.at[z], k_recv.at[zz], {"pb": z * 2 + xx}
        )

    near(lambda z: k_copy(z).start())

    up = {"pb": lax.rem(me + 1, n_pb)}
    down = {"pb": lax.rem(me + n_pb - 1, n_pb)}
    h_up = remote(in_ref.at[rows - 1], halo_in.at[0], h_send.at[0], h_recv.at[0], up)
    h_down = remote(in_ref.at[0], halo_in.at[1], h_send.at[1], h_recv.at[1], down)
    h_up.start()
    h_down.start()

    cin = in_ref.shape[1]

    def spread_rows(value, place):
        for b in range(3):
            in_sh[b * cin : (b + 1) * cin, place * cols : (place + 1) * cols] = moved(
                value, 1 - b
            ).astype(BF16)

    for y in range(rows):
        spread_rows(in_ref[y].astype(F32), y + 1)

    flow_copy.wait_recv()
    spread_flow(flow_in, other)
    remote(q_ref, q_all.at[other], q_send.at[0], q_recv.at[0], {"pb": mate}).wait_recv()
    score_block(zz, other)

    def take(z):
        remote(
            k_all.at[z], k_all.at[z], k_send.at[z], k_recv.at[z], {"pb": z * 2 + xx}
        ).wait_recv()
        for half in range(2):
            score_block(z, half)

    near(take)

    for half in range(2):
        all_peaks = peaks[half * n_z : (half + 1) * n_z]
        peak = jnp.max(all_peaks, axis=0)
        decay = jnp.exp2(all_peaks - peak[None])
        first = 3 * half
        stats[first : first + 1, :] = peak
        stats[first + 1 : first + 2, :] = jnp.sum(
            totals[half * n_z : (half + 1) * n_z] * decay, axis=0
        )
        stats[first + 2 : first + 3, :] = jnp.sum(
            pulls[half * n_z : (half + 1) * n_z] * decay, axis=0
        )
    stat_copies = []
    for i, (dx, dt) in enumerate(team):
        stat_copies.append(
            remote(
                stats, stats_in.at[slot], s_send.at[i], s_recv.at[slot], mate_at(dx, dt)[2]
            )
        )
        stat_copies[-1].start()

    h_up.wait_recv()
    h_down.wait_recv()
    for side, place in ((0, 0), (1, rows + 1)):
        at_end = (me == 0) if side == 0 else (me == n_pb - 1)
        spread_rows(halo_in[side].astype(F32) * jnp.where(at_end, 0.0, 1.0), place)
    f_part[...] = jnp.zeros_like(f_part)

    stats_in[slot] = stats[...]
    for i, (dx, dt) in enumerate(team):
        frm = source_at(dx, dt)
        remote(
            stats, stats_in.at[frm], s_send.at[i], s_recv.at[frm], mate_at(dx, dt)[2]
        ).wait_recv()
    for half in range(2):
        first = 3 * half
        all_peaks = stats_in[:, first : first + 1, :]
        peak = jnp.max(all_peaks, axis=0)
        decay = jnp.exp2(all_peaks - peak[None])
        total = jnp.sum(stats_in[:, first + 1 : first + 2, :] * decay, axis=0)
        weighted = jnp.sum(stats_in[:, first + 2 : first + 3, :] * decay, axis=0)
        finals[half, 0:1, :] = peak
        finals[half, 1:2, :] = weighted / total
        finals[half, 2:3, :] = inv_scale / total

    part = chan // n_ta

    def rows_of(ref, index):
        return ref.at[pl.ds(pl.multiple_of(index * part, part), part), :]

    def feat_half(half):
        def step(origin, _):
            index = half * n_z + origin
            col0, row = place_of(origin)
            scale = jnp.exp2(peaks[index] - finals[half, 0:1, :]) * finals[half, 2:3, :]
            slope = flow_all[half, 0:1, :]
            rest = col0 * slope + row * flow_all[half, 1:2, :] - finals[half, 1:2, :]
            grad = (expo[index] * scale * (iota[...] * slope + rest)).astype(BF16)
            grads[index] = grad
            f_part[half] += matmul(k_all[origin], grad, ((0,), (0,)))
            return 0

        lax.fori_loop(0, n_z, step, 0)
        f_out[half] = f_part[half].astype(BF16)

    f_copies = []

    def send_half(half, dx):
        for i, (ox, dt) in enumerate(team):
            if ox == dx:
                _, t, where = mate_at(ox, dt)
                f_copies.append(
                    remote(
                        rows_of(f_out.at[half], t), f_in.at[slot], f_send.at[i],
                        f_recv.at[slot], where,
                    )
                )
                f_copies[-1].start()

    feat_half(other)
    send_half(other, 1)
    feat_half(xx)
    send_half(xx, 0)

    def target_terms(origin):
        return matmul(grads[origin], q_all[0], ((1,), (0,))) + matmul(
            grads[n_z + origin], q_all[1], ((1,), (0,))
        )

    def g_copy(z):
        return remote(
            g_out.at[z], g_in.at[zz], g_send.at[z], g_recv.at[zz], {"pb": z * 2 + xx}
        )

    def g_step(z):
        g_out[z] = target_terms(z).astype(BF16)
        g_copy(z).start()

    near(g_step)
    g2_ref[...] = target_terms(zz)

    total_f = f_part[xx, pl.ds(pl.multiple_of(grp * part, part), part), :]
    for i, (dx, dt) in enumerate(team):
        frm = source_at(dx, dt)
        remote(
            f_in.at[frm], f_in.at[frm], f_send.at[i], f_recv.at[frm], mate_at(dx, dt)[2]
        ).wait_recv()
        total_f = total_f + f_in[frm].astype(F32)
    feat_ref[pl.ds(pl.multiple_of(grp * part, part), part), :] = total_f.astype(BF16)
    a_copies = []
    for d in range(1, n_ta):
        to = lax.rem(grp + d, n_ta)
        a_copies.append(
            remote(
                rows_of(feat_ref, grp), rows_of(feat_ref, grp), a_send.at[d], a_recv.at[grp],
                {"ta": to},
            )
        )
        a_copies[-1].start()
    for d in range(1, n_ta):
        frm = lax.rem(grp + n_ta - d, n_ta)
        remote(
            rows_of(feat_ref, frm), rows_of(feat_ref, frm), a_send.at[d], a_recv.at[frm],
            {"ta": frm},
        ).wait_recv()

    feat = feat_ref[...]
    width = 3 * cin
    for a in range(3):
        gw_part[a * width : (a + 1) * width, :] = matmul(
            in_sh[:, a * cols : (a + rows) * cols], feat, ((1,), (1,))
        )
    gw_send[...] = gw_part[...].astype(BF16)

    def gw_chunk(ref, index):
        return ref.at[pl.ds(pl.multiple_of(index * gw_rows, gw_rows), gw_rows), :]

    def w_copy(d):
        to = lax.rem(me + d, n_pb)
        return to, remote(
            gw_chunk(gw_send, to), gw_in.at[me], w_send.at[d], w_recv.at[me], {"pb": to}
        )

    def w_start(d, _):
        to = lax.rem(me + d, n_pb)

        @pl.when(to < n_own)
        def _():
            w_copy(d)[1].start()

        return 0

    lax.fori_loop(1, n_pb, w_start, 0)

    spread = matmul(w_ref[...], feat, ((1,), (0,)))
    outs = [None] * (rows + 2)
    for r in range(rows):
        for a in range(3):
            term = None
            for b in range(3):
                first = (a * 3 + b) * cin
                piece = moved(
                    spread[first : first + cin, r * cols : (r + 1) * cols], b - 1
                )
                term = piece if term is None else term + piece
            place = r + a
            outs[place] = term if outs[place] is None else outs[place] + term
    edge_out[0] = outs[rows + 1]
    edge_out[1] = outs[0]
    e_up = remote(edge_out.at[0], edge_in.at[0], e_send.at[0], e_recv.at[0], up)
    e_down = remote(edge_out.at[1], edge_in.at[1], e_send.at[1], e_recv.at[1], down)
    e_up.start()
    e_down.start()
    for y in range(rows):
        gi_ref[y] = outs[y + 1]

    @pl.when(me < n_own)
    def _():
        first = pl.multiple_of(me * gw_rows, gw_rows)
        gw_all[pl.ds(first, gw_rows), :] = gw_part[pl.ds(first, gw_rows), :]

        def add(d, _):
            frm = lax.rem(me + n_pb - d, n_pb)
            remote(
                gw_in.at[frm], gw_in.at[frm], w_send.at[d], w_recv.at[frm], {"pb": frm}
            ).wait_recv()
            gw_all[pl.ds(first, gw_rows), :] += gw_in[frm].astype(F32)
            return 0

        lax.fori_loop(1, n_pb, add, 0)

        def give(d, _):
            to = lax.rem(me + d, n_pb)
            remote(
                gw_chunk(gw_all, me), gw_chunk(gw_all, me), v_send.at[d], v_recv.at[me],
                {"pb": to},
            ).start()
            return 0

        lax.fori_loop(1, n_pb, give, 0)

    def g_add(z):
        remote(
            g_in.at[z], g_in.at[z], g_send.at[z], g_recv.at[z], {"pb": z * 2 + xx}
        ).wait_recv()
        g2_ref[...] += g_in[z].astype(F32)

    near(g_add)

    e_up.wait_recv()
    e_down.wait_recv()
    gi_ref[0] += edge_in[0] * jnp.where(me == 0, 0.0, 1.0)
    gi_ref[rows - 1] += edge_in[1] * jnp.where(me == n_pb - 1, 0.0, 1.0)

    def v_wait(d, _):
        frm = lax.rem(me + n_pb - d, n_pb)

        @pl.when(frm < n_own)
        def _():
            remote(
                gw_chunk(gw_all, frm), gw_chunk(gw_all, frm), v_send.at[d], v_recv.at[frm],
                {"pb": frm},
            ).wait_recv()

        return 0

    lax.fori_loop(1, n_pb, v_wait, 0)
    gw_ref[...] = gw_all[...]

    for copy in (
        q_copy, flow_copy, h_up, h_down, e_up, e_down, *stat_copies, *f_copies, *a_copies
    ):
        copy.wait_send()

    def gone(z):
        k_copy(z).wait_send()
        g_copy(z).wait_send()

    near(gone)

    def drain(d, _):
        @pl.when(lax.rem(me + d, n_pb) < n_own)
        def _():
            w_copy(d)[1].wait_send()

        @pl.when(me < n_own)
        def _():
            remote(
                gw_chunk(gw_all, me), gw_chunk(gw_all, me), v_send.at[d], v_recv.at[me],
                {"pb": lax.rem(me + d, n_pb)},
            ).wait_send()

        return 0

    lax.fori_loop(1, n_pb, drain, 0)


def per_device(n_pb, n_ta, feat_one, feat_two, cot_flow, enc_input, enc_weight):
    rows, cols, chan = feat_one.shape
    n_q = rows * cols
    tgt = feat_two.shape[1]
    cin = enc_input.shape[1]
    taps = 9 * cin
    assert n_pb % 2 == 0 and FRAME_COLS % tgt == 0 and taps % 16 == 0
    gw_rows = 16 * pl.cdiv(taps // 16, n_pb)
    assert taps % gw_rows == 0
    vmem = pl.BlockSpec(memory_space=pltpu.VMEM)
    dma = pltpu.SemaphoreType.DMA
    n_z = n_pb // 2
    outs = pl.pallas_call(
        functools.partial(kernel, n_pb, n_ta, rows, cols, gw_rows),
        out_shape=(
            jax.ShapeDtypeStruct((tgt, chan), F32),
            jax.ShapeDtypeStruct((rows, cin, cols), F32),
            jax.ShapeDtypeStruct((taps, chan), F32),
        ),
        in_specs=[vmem] * 5,
        out_specs=(vmem,) * 3,
        scratch_shapes=[
            pltpu.VMEM((2, n_q, chan), BF16),
            pltpu.VMEM((2, rows, cols), F32),
            pltpu.VMEM((2, 8, n_q), F32),
            pltpu.VMEM((n_z, tgt, chan), BF16),
            pltpu.VMEM((n_pb, tgt, n_q), F32),
            pltpu.VMEM((n_pb, tgt, n_q), BF16),
            pltpu.VMEM((tgt, n_q), F32),
            pltpu.VMEM((n_pb, 1, n_q), F32),
            pltpu.VMEM((n_pb, 1, n_q), F32),
            pltpu.VMEM((n_pb, 1, n_q), F32),
            pltpu.VMEM((8, n_q), F32),
            pltpu.VMEM((2 * n_ta, 8, n_q), F32),
            pltpu.VMEM((2, 8, n_q), F32),
            pltpu.VMEM((n_z, tgt, chan), BF16),
            pltpu.VMEM((n_z, tgt, chan), BF16),
            pltpu.VMEM((2, chan, n_q), F32),
            pltpu.VMEM((2, chan, n_q), BF16),
            pltpu.VMEM((2 * n_ta, chan // n_ta, n_q), BF16),
            pltpu.VMEM((chan, n_q), BF16),
            pltpu.VMEM((2, cin, cols), BF16),
            pltpu.VMEM((3 * cin, (rows + 2) * cols), BF16),
            pltpu.VMEM((2, cin, cols), F32),
            pltpu.VMEM((2, cin, cols), F32),
            pltpu.VMEM((taps, chan), F32),
            pltpu.VMEM((taps, chan), BF16),
            pltpu.VMEM((n_pb, gw_rows, chan), BF16),
            pltpu.VMEM((taps, chan), F32),
            dma((2,)), dma((2,)),
            dma((n_z,)), dma((n_z,)),
            dma((2 * n_ta,)), dma((2 * n_ta,)),
            dma((n_z,)), dma((n_z,)),
            dma((2 * n_ta,)), dma((2 * n_ta,)),
            dma((n_ta,)), dma((n_ta,)),
            dma((2,)), dma((2,)),
            dma((2,)), dma((2,)),
            dma((n_pb,)), dma((n_pb,)),
            dma((n_pb,)), dma((n_pb,)),
        ],
        compiler_params=pltpu.CompilerParams(collective_id=0, has_side_effects=True),
        name="matching",
    )(
        feat_one.reshape(n_q, chan),
        feat_two[0],
        cot_flow,
        enc_input,
        enc_weight.reshape(taps, chan),
    )
    return (
        outs[0][None],
        outs[1],
        outs[2].reshape(3, 3, cin, chan),
    )


def solution(mesh):
    in_specs = (
        P("pb", None, None),
        P("ta", "pb", None),
        P(None, "pb", None),
        P("pb", "ta", None),
        P(None, None, "ta", None),
    )
    out_specs = (P("ta", "pb", None), P("pb", "ta", None), P(None, None, "ta", None))
    body = functools.partial(per_device, mesh.shape["pb"], mesh.shape["ta"])
    return jax.shard_map(
        body, mesh=mesh, in_specs=in_specs, out_specs=out_specs, check_vma=False
    )
```

```python
import functools
import math

import jax
import jax.numpy as jnp
from jax import lax
from jax.experimental import pallas as pl
from jax.experimental.pallas import tpu as pltpu
from jax.sharding import PartitionSpec as P

FRAME_COLS = 512
MESH = pl.DeviceIdType.MESH
F32 = jnp.float32
BF16 = jnp.bfloat16


def remote(src, dst, send_sem, recv_sem, where):
    return pltpu.make_async_remote_copy(
        src_ref=src,
        dst_ref=dst,
        send_sem=send_sem,
        recv_sem=recv_sem,
        device_id=where,
        device_id_type=MESH,
    )


def matmul(left, right, dims):
    return lax.dot_general(left, right, (dims, ((), ())), preferred_element_type=F32)


def moved(value, step):
    if step == 0:
        return value
    width = value.shape[1]
    lane = lax.broadcasted_iota(jnp.int32, value.shape, 1)
    rolled = pltpu.roll(value, step % width, 1)
    edge = 0 if step > 0 else width - 1
    return jnp.where(lane == edge, 0.0, rolled)


def kernel(
    n_pb, n_ta, rows, cols, gw_rows,
    q_hbm, k_hbm, flow_hbm, in_hbm, w_hbm,
    g2_ref, gi_ref, gw_ref,
    flow_ref, in_ref, w_ref, load_sem, q_all, flow_in, flow_all, k_all, expo, grads, iota, peaks, totals, pulls, stats, stats_in,
    finals, g_out, g_in, f_part, f_out, f_in, feat_ref, halo_in, in_sh,
    edge_out, edge_in, gw_part, gw_send, gw_in, gw_sum, gw_all,
    q_send, q_recv, k_send, k_recv, s_send, s_recv, g_send, g_recv,
    f_send, f_recv, a_send, a_recv, h_send, h_recv, e_send, e_recv,
    w_send, w_recv, v_send, v_recv,
):
    me = lax.axis_index("pb")
    grp = lax.axis_index("ta")
    zz, xx = me // 2, me % 2
    n_z = n_pb // 2
    other = 1 - xx
    mate = zz * 2 + other
    n_q, chan = q_hbm.shape
    tgt = k_hbm.shape[0]
    n_own = n_pb // 2
    own_first = n_pb // 4
    own = me - own_first
    is_own = jnp.logical_and(own >= 0, own < n_own)

    def gw_start(index):
        last = gw_part.shape[0] - gw_rows
        return pl.multiple_of(index * last // (n_own - 1) // 16 * 16, 16)

    inv_scale = 1.0 / math.sqrt(chan)
    unit = inv_scale / math.log(2.0)
    team = [(dx, dt) for dx in (1, 0) for dt in range(n_ta - 1, -1, -1) if dx or dt]

    def mate_at(dx, dt):
        x, t = lax.rem(xx + dx, 2), lax.rem(grp + dt, n_ta)
        return x, t, {"pb": zz * 2 + x, "ta": t}

    def source_at(dx, dt):
        x, t = lax.rem(xx + dx, 2), lax.rem(grp + n_ta - dt, n_ta)
        return x * n_ta + t

    slot = xx * n_ta + grp

    barrier = pltpu.get_barrier_semaphore()

    def greet(d, _):
        pl.semaphore_signal(
            barrier, inc=1, device_id={"pb": lax.rem(me + d, n_pb)}, device_id_type=MESH
        )
        return 0

    lax.fori_loop(1, n_pb, greet, 0)
    for dx, dt in team:
        if dt:
            pl.semaphore_signal(
                barrier, inc=1, device_id=mate_at(dx, dt)[2], device_id_type=MESH
            )

    q_ref, k_ref = q_all.at[xx], k_all.at[zz]
    loads = [
        pltpu.make_async_copy(src, dst, load_sem.at[i])
        for i, (src, dst) in enumerate(
            (
                (k_hbm, k_ref), (q_hbm, q_ref), (flow_hbm, flow_ref), (in_hbm, in_ref),
                (w_hbm, w_ref),
            )
        )
    ]
    for load in loads:
        load.start()

    def spread_flow(ref, half):
        for r in range(rows):
            for comp in range(2):
                flow_all[half, comp : comp + 1, r * cols : (r + 1) * cols] = ref[
                    comp, r : r + 1, :
                ]

    def place_of(origin):
        k0 = (grp * n_pb + origin * 2 + xx) * tgt
        col0 = (lax.rem(k0, FRAME_COLS) - FRAME_COLS // 2).astype(F32)
        return col0, (k0 // FRAME_COLS).astype(F32)

    def score_block(origin, half):
        raw = matmul(k_all[origin], q_all[half], ((1,), (1,)))
        peak = jnp.max(raw, axis=0, keepdims=True) * unit
        value = jnp.exp2(raw * unit - peak)
        index = half * n_z + origin
        expo[index] = value
        col0, row = place_of(origin)
        total = jnp.sum(value, axis=0, keepdims=True)
        along = jnp.sum(value * iota[...], axis=0, keepdims=True)
        peaks[index] = peak
        totals[index] = total
        pulls[index] = flow_all[half, 0:1, :] * (along + col0 * total) + flow_all[
            half, 1:2, :
        ] * (row * total)

    iota[...] = lax.broadcasted_iota(jnp.int32, (tgt, n_q), 0).astype(F32)
    for load in loads:
        load.wait()
    spread_flow(flow_ref, xx)
    score_block(zz, xx)
    pl.semaphore_wait(barrier, n_pb - 1 + 2 * (n_ta - 1))

    q_copy = remote(q_ref, q_all.at[xx], q_send.at[0], q_recv.at[0], {"pb": mate})
    flow_copy = remote(flow_ref, flow_in, q_send.at[1], q_recv.at[1], {"pb": mate})
    q_copy.start()
    flow_copy.start()

    def near(fn):
        def step(t, _):
            dist = t // 2 + 1
            z = zz + dist * (1 - 2 * (t % 2))

            @pl.when(jnp.logical_and(z >= 0, z < n_z))
            def _():
                fn(z)

            return 0

        lax.fori_loop(0, 2 * (n_z - 1), step, 0)

    def k_copy(z):
        return remote(
            k_ref, k_all.at[zz], k_send.at[z], k_recv.at[zz], {"pb": z * 2 + xx}
        )

    near(lambda z: k_copy(z).start())

    up = {"pb": lax.rem(me + 1, n_pb)}
    down = {"pb": lax.rem(me + n_pb - 1, n_pb)}
    h_up = remote(in_ref.at[rows - 1], halo_in.at[0], h_send.at[0], h_recv.at[0], up)
    h_down = remote(in_ref.at[0], halo_in.at[1], h_send.at[1], h_recv.at[1], down)
    h_up.start()
    h_down.start()

    cin = in_ref.shape[1]

    def spread_rows(value, place):
        for b in range(3):
            in_sh[b * cin : (b + 1) * cin, place * cols : (place + 1) * cols] = moved(
                value, 1 - b
            ).astype(BF16)

    for y in range(rows):
        spread_rows(in_ref[y].astype(F32), y + 1)

    flow_copy.wait_recv()
    spread_flow(flow_in, other)
    remote(q_all.at[other], q_all.at[other], q_send.at[0], q_recv.at[0], {"pb": mate}).wait_recv()
    score_block(zz, other)

    def take(z):
        remote(
            k_all.at[z], k_all.at[z], k_send.at[z], k_recv.at[z], {"pb": z * 2 + xx}
        ).wait_recv()
        for half in range(2):
            score_block(z, half)

    near(take)

    for half in range(2):
        all_peaks = peaks[half * n_z : (half + 1) * n_z]
        peak = jnp.max(all_peaks, axis=0)
        decay = jnp.exp2(all_peaks - peak[None])
        first = 3 * half
        stats[first : first + 1, :] = peak
        stats[first + 1 : first + 2, :] = jnp.sum(
            totals[half * n_z : (half + 1) * n_z] * decay, axis=0
        )
        stats[first + 2 : first + 3, :] = jnp.sum(
            pulls[half * n_z : (half + 1) * n_z] * decay, axis=0
        )
    stat_copies = []
    for i, (dx, dt) in enumerate(team):
        stat_copies.append(
            remote(
                stats, stats_in.at[slot], s_send.at[i], s_recv.at[slot], mate_at(dx, dt)[2]
            )
        )
        stat_copies[-1].start()

    h_up.wait_recv()
    h_down.wait_recv()
    for side, place in ((0, 0), (1, rows + 1)):
        at_end = (me == 0) if side == 0 else (me == n_pb - 1)
        spread_rows(halo_in[side].astype(F32) * jnp.where(at_end, 0.0, 1.0), place)
    f_part[...] = jnp.zeros_like(f_part)

    stats_in[slot] = stats[...]
    for i, (dx, dt) in enumerate(team):
        frm = source_at(dx, dt)
        remote(
            stats, stats_in.at[frm], s_send.at[i], s_recv.at[frm], mate_at(dx, dt)[2]
        ).wait_recv()
    for half in range(2):
        first = 3 * half
        all_peaks = stats_in[:, first : first + 1, :]
        peak = jnp.max(all_peaks, axis=0)
        decay = jnp.exp2(all_peaks - peak[None])
        total = jnp.sum(stats_in[:, first + 1 : first + 2, :] * decay, axis=0)
        weighted = jnp.sum(stats_in[:, first + 2 : first + 3, :] * decay, axis=0)
        finals[half, 0:1, :] = peak
        finals[half, 1:2, :] = weighted / total
        finals[half, 2:3, :] = inv_scale / total

    part = chan // n_ta

    def rows_of(ref, index):
        return ref.at[pl.ds(pl.multiple_of(index * part, part), part), :]

    def feat_half(half):
        def step(origin, _):
            index = half * n_z + origin
            col0, row = place_of(origin)
            scale = jnp.exp2(peaks[index] - finals[half, 0:1, :]) * finals[half, 2:3, :]
            slope = flow_all[half, 0:1, :]
            rest = col0 * slope + row * flow_all[half, 1:2, :] - finals[half, 1:2, :]
            grad = (expo[index] * scale * (iota[...] * slope + rest)).astype(BF16)
            grads[index] = grad
            f_part[half] += matmul(k_all[origin], grad, ((0,), (0,)))
            return 0

        lax.fori_loop(0, n_z, step, 0)
        f_out[half] = f_part[half].astype(BF16)

    f_copies = []

    def send_half(half, dx):
        for i, (ox, dt) in enumerate(team):
            if ox == dx:
                _, t, where = mate_at(ox, dt)
                f_copies.append(
                    remote(
                        rows_of(f_out.at[half], t), f_in.at[slot], f_send.at[i],
                        f_recv.at[slot], where,
                    )
                )
                f_copies[-1].start()

    feat_half(other)
    send_half(other, 1)
    feat_half(xx)
    send_half(xx, 0)

    def target_terms(origin):
        return matmul(grads[origin], q_all[0], ((1,), (0,))) + matmul(
            grads[n_z + origin], q_all[1], ((1,), (0,))
        )

    def g_copy(z):
        return remote(
            g_out.at[z], g_in.at[zz], g_send.at[z], g_recv.at[zz], {"pb": z * 2 + xx}
        )

    def g_step(z):
        g_out[z] = target_terms(z).astype(BF16)
        g_copy(z).start()

    near(g_step)
    g2_ref[...] = target_terms(zz)

    total_f = f_part[xx, pl.ds(pl.multiple_of(grp * part, part), part), :]
    for i, (dx, dt) in enumerate(team):
        frm = source_at(dx, dt)
        remote(
            f_in.at[frm], f_in.at[frm], f_send.at[i], f_recv.at[frm], mate_at(dx, dt)[2]
        ).wait_recv()
        total_f = total_f + f_in[frm].astype(F32)
    feat_ref[pl.ds(pl.multiple_of(grp * part, part), part), :] = total_f.astype(BF16)
    a_copies = []
    for d in range(1, n_ta):
        to = lax.rem(grp + d, n_ta)
        a_copies.append(
            remote(
                rows_of(feat_ref, grp), rows_of(feat_ref, grp), a_send.at[d], a_recv.at[grp],
                {"ta": to},
            )
        )
        a_copies[-1].start()
    for d in range(1, n_ta):
        frm = lax.rem(grp + n_ta - d, n_ta)
        remote(
            rows_of(feat_ref, frm), rows_of(feat_ref, frm), a_send.at[d], a_recv.at[frm],
            {"ta": frm},
        ).wait_recv()

    feat = feat_ref[...]
    width = 3 * cin
    for a in range(3):
        gw_part[a * width : (a + 1) * width, :] = matmul(
            in_sh[:, a * cols : (a + rows) * cols], feat, ((1,), (1,))
        )
    gw_send[...] = gw_part[...].astype(BF16)

    def w_copy(index):
        return remote(
            gw_send.at[pl.ds(gw_start(index), gw_rows), :], gw_in.at[me],
            w_send.at[index], w_recv.at[me], {"pb": own_first + index},
        )

    def to_owners(fn):
        def step(index, _):
            @pl.when(index != own)
            def _():
                fn(index)

            return 0

        lax.fori_loop(0, n_own, step, 0)

    to_owners(lambda index: w_copy(index).start())

    spread = matmul(w_ref[...], feat, ((1,), (0,)))
    outs = [None] * (rows + 2)
    for r in range(rows):
        for a in range(3):
            term = None
            for b in range(3):
                first = (a * 3 + b) * cin
                piece = moved(
                    spread[first : first + cin, r * cols : (r + 1) * cols], b - 1
                )
                term = piece if term is None else term + piece
            place = r + a
            outs[place] = term if outs[place] is None else outs[place] + term
    edge_out[0] = outs[rows + 1]
    edge_out[1] = outs[0]
    e_up = remote(edge_out.at[0], edge_in.at[0], e_send.at[0], e_recv.at[0], up)
    e_down = remote(edge_out.at[1], edge_in.at[1], e_send.at[1], e_recv.at[1], down)
    e_up.start()
    e_down.start()
    for y in range(rows):
        gi_ref[y] = outs[y + 1]

    def v_copy(d):
        return remote(
            gw_sum, gw_all.at[own], v_send.at[d], v_recv.at[own],
            {"pb": lax.rem(me + d, n_pb)},
        )

    @pl.when(is_own)
    def _():
        def add(d, total):
            frm = lax.rem(me + n_pb - d, n_pb)
            remote(
                gw_in.at[frm], gw_in.at[frm], w_send.at[0], w_recv.at[frm], {"pb": frm}
            ).wait_recv()
            return total + gw_in[frm].astype(F32)

        total = lax.fori_loop(1, n_pb, add, gw_part[pl.ds(gw_start(own), gw_rows), :])
        gw_sum[...] = total.astype(BF16)

        def give(d, _):
            v_copy(d).start()
            return 0

        lax.fori_loop(1, n_pb, give, 0)
        gw_all[own] = gw_sum[...]

    def g_add(z):
        remote(
            g_in.at[z], g_in.at[z], g_send.at[z], g_recv.at[z], {"pb": z * 2 + xx}
        ).wait_recv()
        g2_ref[...] += g_in[z].astype(F32)

    near(g_add)

    e_up.wait_recv()
    e_down.wait_recv()
    gi_ref[0] += edge_in[0] * jnp.where(me == 0, 0.0, 1.0)
    gi_ref[rows - 1] += edge_in[1] * jnp.where(me == n_pb - 1, 0.0, 1.0)

    def v_wait(index):
        remote(
            gw_all.at[index], gw_all.at[index], v_send.at[0], v_recv.at[index],
            {"pb": own_first + index},
        ).wait_recv()

    to_owners(v_wait)

    def write(index, _):
        gw_ref[pl.ds(gw_start(index), gw_rows), :] = gw_all[index].astype(F32)
        return 0

    lax.fori_loop(0, n_own, write, 0)

    for copy in (
        q_copy, flow_copy, h_up, h_down, e_up, e_down, *stat_copies, *f_copies, *a_copies
    ):
        copy.wait_send()

    def gone(z):
        k_copy(z).wait_send()
        g_copy(z).wait_send()

    near(gone)

    to_owners(lambda index: w_copy(index).wait_send())

    @pl.when(is_own)
    def _():
        def drain(d, _):
            v_copy(d).wait_send()
            return 0

        lax.fori_loop(1, n_pb, drain, 0)


def place(g2_in, gi_in, gw_in, g2_ref, gi_ref, gw_ref, sem):
    copies = [
        pltpu.make_async_copy(src, dst, sem.at[i])
        for i, (src, dst) in enumerate(
            ((g2_in, g2_ref), (gi_in, gi_ref), (gw_in, gw_ref))
        )
    ]
    for copy in copies:
        copy.start()
    for copy in copies:
        copy.wait()


def per_device(n_pb, n_ta, feat_one, feat_two, cot_flow, enc_input, enc_weight):
    rows, cols, chan = feat_one.shape
    n_q = rows * cols
    tgt = feat_two.shape[1]
    cin = enc_input.shape[1]
    taps = 9 * cin
    assert n_pb % 4 == 0 and FRAME_COLS % tgt == 0 and taps % 16 == 0
    gw_rows = 16 * pl.cdiv(taps // 16, n_pb // 2)
    vmem = pl.BlockSpec(memory_space=pltpu.VMEM)
    dma = pltpu.SemaphoreType.DMA
    n_z = n_pb // 2
    shapes = ((tgt, chan), (rows, cin, cols), (taps, chan))
    outs = pl.pallas_call(
        functools.partial(kernel, n_pb, n_ta, rows, cols, gw_rows),
        out_shape=tuple(pltpu.VMEM(shape, F32) for shape in shapes),
        in_specs=[pl.BlockSpec(memory_space=pl.ANY)] * 5,
        out_specs=(vmem,) * 3,
        scratch_shapes=[
            pltpu.VMEM((2, rows, cols), F32),
            pltpu.VMEM((rows, cin, cols), BF16),
            pltpu.VMEM((taps, chan), BF16),
            dma((5,)),
            pltpu.VMEM((2, n_q, chan), BF16),
            pltpu.VMEM((2, rows, cols), F32),
            pltpu.VMEM((2, 8, n_q), F32),
            pltpu.VMEM((n_z, tgt, chan), BF16),
            pltpu.VMEM((n_pb, tgt, n_q), F32),
            pltpu.VMEM((n_pb, tgt, n_q), BF16),
            pltpu.VMEM((tgt, n_q), F32),
            pltpu.VMEM((n_pb, 1, n_q), F32),
            pltpu.VMEM((n_pb, 1, n_q), F32),
            pltpu.VMEM((n_pb, 1, n_q), F32),
            pltpu.VMEM((8, n_q), F32),
            pltpu.VMEM((2 * n_ta, 8, n_q), F32),
            pltpu.VMEM((2, 8, n_q), F32),
            pltpu.VMEM((n_z, tgt, chan), BF16),
            pltpu.VMEM((n_z, tgt, chan), BF16),
            pltpu.VMEM((2, chan, n_q), F32),
            pltpu.VMEM((2, chan, n_q), BF16),
            pltpu.VMEM((2 * n_ta, chan // n_ta, n_q), BF16),
            pltpu.VMEM((chan, n_q), BF16),
            pltpu.VMEM((2, cin, cols), BF16),
            pltpu.VMEM((3 * cin, (rows + 2) * cols), BF16),
            pltpu.VMEM((2, cin, cols), F32),
            pltpu.VMEM((2, cin, cols), F32),
            pltpu.VMEM((taps, chan), F32),
            pltpu.VMEM((taps, chan), BF16),
            pltpu.VMEM((n_pb, gw_rows, chan), BF16),
            pltpu.VMEM((gw_rows, chan), BF16),
            pltpu.VMEM((n_pb // 2, gw_rows, chan), BF16),
            dma((2,)), dma((2,)),
            dma((n_z,)), dma((n_z,)),
            dma((2 * n_ta,)), dma((2 * n_ta,)),
            dma((n_z,)), dma((n_z,)),
            dma((2 * n_ta,)), dma((2 * n_ta,)),
            dma((n_ta,)), dma((n_ta,)),
            dma((2,)), dma((2,)),
            dma((2,)), dma((2,)),
            dma((n_pb // 2,)), dma((n_pb,)),
            dma((n_pb,)), dma((n_pb // 2,)),
        ],
        compiler_params=pltpu.CompilerParams(collective_id=0, has_side_effects=True),
        name="matching",
    )(
        feat_one.reshape(n_q, chan),
        feat_two[0],
        cot_flow,
        enc_input,
        enc_weight.reshape(taps, chan),
    )
    outs = pl.pallas_call(
        place,
        out_shape=tuple(jax.ShapeDtypeStruct(shape, F32) for shape in shapes),
        in_specs=[vmem] * 3,
        out_specs=(pl.BlockSpec(memory_space=pl.ANY),) * 3,
        scratch_shapes=[dma((3,))],
        name="place",
    )(*(pltpu.with_memory_space_constraint(out, pltpu.VMEM) for out in outs))
    return (
        outs[0][None],
        outs[1],
        outs[2].reshape(3, 3, cin, chan),
    )


def solution(mesh):
    in_specs = (
        P("pb", None, None),
        P("ta", "pb", None),
        P(None, "pb", None),
        P("pb", "ta", None),
        P(None, None, "ta", None),
    )
    out_specs = (P("ta", "pb", None), P("pb", "ta", None), P(None, None, "ta", None))
    body = functools.partial(per_device, mesh.shape["pb"], mesh.shape["ta"])
    return jax.shard_map(
        body, mesh=mesh, in_specs=in_specs, out_specs=out_specs, check_vma=False
    )
```

```python
import functools
import math

import jax
import jax.numpy as jnp
from jax import lax
from jax.experimental import pallas as pl
from jax.experimental.pallas import tpu as pltpu
from jax.sharding import PartitionSpec as P

FRAME_COLS = 512
MESH = pl.DeviceIdType.MESH
F32 = jnp.float32
BF16 = jnp.bfloat16


def remote(src, dst, send_sem, recv_sem, where):
    return pltpu.make_async_remote_copy(
        src_ref=src,
        dst_ref=dst,
        send_sem=send_sem,
        recv_sem=recv_sem,
        device_id=where,
        device_id_type=MESH,
    )


def matmul(left, right, dims):
    return lax.dot_general(left, right, (dims, ((), ())), preferred_element_type=F32)


def moved(value, step):
    if step == 0:
        return value
    width = value.shape[1]
    lane = lax.broadcasted_iota(jnp.int32, value.shape, 1)
    rolled = pltpu.roll(value, step % width, 1)
    edge = 0 if step > 0 else width - 1
    return jnp.where(lane == edge, 0.0, rolled)


def kernel(
    n_pb, n_ta, rows, cols, gw_rows,
    q_hbm, k_hbm, flow_hbm, in_hbm, w_hbm,
    g2_ref, gi_ref, gw_ref,
    flow_ref, in_ref, w_ref, load_sem, q_all, flow_in, flow_all, k_all, expo, grads, iota, peaks, totals, pulls, stats, stats_in,
    finals, g_out, g_in, f_part, f_out, f_in, feat_ref, halo_in, in_sh,
    edge_out, edge_in, gw_part, gw_send, gw_in, gw_sum, gw_all,
    q_send, q_recv, k_send, k_recv, s_send, s_recv, g_send, g_recv,
    f_send, f_recv, a_send, a_recv, h_send, h_recv, e_send, e_recv,
    w_send, w_recv, v_send, v_recv,
):
    me = lax.axis_index("pb")
    grp = lax.axis_index("ta")
    zz, xx = me // 2, me % 2
    n_z = n_pb // 2
    other = 1 - xx
    mate = zz * 2 + other
    n_q, chan = q_hbm.shape
    tgt = k_hbm.shape[0]
    n_own = n_pb // 2
    own_first = n_pb // 4
    own = me - own_first
    is_own = jnp.logical_and(own >= 0, own < n_own)

    def gw_start(index):
        last = gw_part.shape[0] - gw_rows
        return pl.multiple_of(index * last // (n_own - 1) // 16 * 16, 16)

    inv_scale = 1.0 / math.sqrt(chan)
    unit = inv_scale / math.log(2.0)
    team = [(dx, dt) for dx in (1, 0) for dt in range(n_ta - 1, -1, -1) if dx or dt]

    def mate_at(dx, dt):
        x, t = lax.rem(xx + dx, 2), lax.rem(grp + dt, n_ta)
        return x, t, {"pb": zz * 2 + x, "ta": t}

    def source_at(dx, dt):
        x, t = lax.rem(xx + dx, 2), lax.rem(grp + n_ta - dt, n_ta)
        return x * n_ta + t

    slot = xx * n_ta + grp

    barrier = pltpu.get_barrier_semaphore()

    def greet(d, _):
        pl.semaphore_signal(
            barrier, inc=1, device_id={"pb": lax.rem(me + d, n_pb)}, device_id_type=MESH
        )
        return 0

    lax.fori_loop(1, n_pb, greet, 0)
    for dx, dt in team:
        if dt:
            pl.semaphore_signal(
                barrier, inc=1, device_id=mate_at(dx, dt)[2], device_id_type=MESH
            )

    q_ref, k_ref = q_all.at[xx], k_all.at[zz]
    loads = [
        pltpu.make_async_copy(src, dst, load_sem.at[i])
        for i, (src, dst) in enumerate(
            (
                (k_hbm, k_ref), (q_hbm, q_ref), (flow_hbm, flow_ref), (in_hbm, in_ref),
                (w_hbm, w_ref),
            )
        )
    ]
    for load in loads:
        load.start()

    def spread_flow(ref, half):
        for r in range(rows):
            for comp in range(2):
                flow_all[half, comp : comp + 1, r * cols : (r + 1) * cols] = ref[
                    comp, r : r + 1, :
                ]

    def place_of(origin):
        k0 = (grp * n_pb + origin * 2 + xx) * tgt
        col0 = (lax.rem(k0, FRAME_COLS) - FRAME_COLS // 2).astype(F32)
        return col0, (k0 // FRAME_COLS).astype(F32)

    def score_block(origin, half):
        raw = matmul(k_all[origin], q_all[half], ((1,), (1,)))
        peak = jnp.max(raw, axis=0, keepdims=True) * unit
        value = jnp.exp2(raw * unit - peak)
        index = half * n_z + origin
        expo[index] = value
        col0, row = place_of(origin)
        total = jnp.sum(value, axis=0, keepdims=True)
        along = jnp.sum(value * iota[...], axis=0, keepdims=True)
        peaks[index] = peak
        totals[index] = total
        pulls[index] = flow_all[half, 0:1, :] * (along + col0 * total) + flow_all[
            half, 1:2, :
        ] * (row * total)

    iota[...] = lax.broadcasted_iota(jnp.int32, (tgt, n_q), 0).astype(F32)
    for load in loads:
        load.wait()
    spread_flow(flow_ref, xx)
    score_block(zz, xx)
    pl.semaphore_wait(barrier, n_pb - 1 + 2 * (n_ta - 1))

    q_copy = remote(q_ref, q_all.at[xx], q_send.at[0], q_recv.at[0], {"pb": mate})
    flow_copy = remote(flow_ref, flow_in, q_send.at[1], q_recv.at[1], {"pb": mate})
    q_copy.start()
    flow_copy.start()

    def near(fn):
        def step(t, _):
            dist = t // 2 + 1
            z = zz + dist * (1 - 2 * (t % 2))

            @pl.when(jnp.logical_and(z >= 0, z < n_z))
            def _():
                fn(z)

            return 0

        lax.fori_loop(0, 2 * (n_z - 1), step, 0)

    def k_copy(z):
        return remote(
            k_ref, k_all.at[zz], k_send.at[z], k_recv.at[zz], {"pb": z * 2 + xx}
        )

    near(lambda z: k_copy(z).start())

    up = {"pb": lax.rem(me + 1, n_pb)}
    down = {"pb": lax.rem(me + n_pb - 1, n_pb)}
    h_up = remote(in_ref.at[rows - 1], halo_in.at[0], h_send.at[0], h_recv.at[0], up)
    h_down = remote(in_ref.at[0], halo_in.at[1], h_send.at[1], h_recv.at[1], down)
    h_up.start()
    h_down.start()

    cin = in_ref.shape[1]

    def spread_rows(value, place):
        for b in range(3):
            in_sh[b * cin : (b + 1) * cin, place * cols : (place + 1) * cols] = moved(
                value, 1 - b
            ).astype(BF16)

    for y in range(rows):
        spread_rows(in_ref[y].astype(F32), y + 1)

    flow_copy.wait_recv()
    spread_flow(flow_in, other)
    remote(q_all.at[other], q_all.at[other], q_send.at[0], q_recv.at[0], {"pb": mate}).wait_recv()
    score_block(zz, other)

    def take(z):
        remote(
            k_all.at[z], k_all.at[z], k_send.at[z], k_recv.at[z], {"pb": z * 2 + xx}
        ).wait_recv()
        for half in range(2):
            score_block(z, half)

    near(take)

    for half in range(2):
        all_peaks = peaks[half * n_z : (half + 1) * n_z]
        peak = jnp.max(all_peaks, axis=0)
        decay = jnp.exp2(all_peaks - peak[None])
        first = 3 * half
        stats[first : first + 1, :] = peak
        stats[first + 1 : first + 2, :] = jnp.sum(
            totals[half * n_z : (half + 1) * n_z] * decay, axis=0
        )
        stats[first + 2 : first + 3, :] = jnp.sum(
            pulls[half * n_z : (half + 1) * n_z] * decay, axis=0
        )
    stat_copies = []
    for i, (dx, dt) in enumerate(team):
        stat_copies.append(
            remote(
                stats, stats_in.at[slot], s_send.at[i], s_recv.at[slot], mate_at(dx, dt)[2]
            )
        )
        stat_copies[-1].start()

    h_up.wait_recv()
    h_down.wait_recv()
    for side, place in ((0, 0), (1, rows + 1)):
        at_end = (me == 0) if side == 0 else (me == n_pb - 1)
        spread_rows(halo_in[side].astype(F32) * jnp.where(at_end, 0.0, 1.0), place)
    f_part[...] = jnp.zeros_like(f_part)

    stats_in[slot] = stats[...]
    for i, (dx, dt) in enumerate(team):
        frm = source_at(dx, dt)
        remote(
            stats, stats_in.at[frm], s_send.at[i], s_recv.at[frm], mate_at(dx, dt)[2]
        ).wait_recv()
    for half in range(2):
        first = 3 * half
        all_peaks = stats_in[:, first : first + 1, :]
        peak = jnp.max(all_peaks, axis=0)
        decay = jnp.exp2(all_peaks - peak[None])
        total = jnp.sum(stats_in[:, first + 1 : first + 2, :] * decay, axis=0)
        weighted = jnp.sum(stats_in[:, first + 2 : first + 3, :] * decay, axis=0)
        finals[half, 0:1, :] = peak
        finals[half, 1:2, :] = weighted / total
        finals[half, 2:3, :] = inv_scale / total

    part = chan // n_ta

    def rows_of(ref, index):
        return ref.at[pl.ds(pl.multiple_of(index * part, part), part), :]

    def feat_half(half):
        def step(origin, _):
            index = half * n_z + origin
            col0, row = place_of(origin)
            scale = jnp.exp2(peaks[index] - finals[half, 0:1, :]) * finals[half, 2:3, :]
            slope = flow_all[half, 0:1, :]
            rest = col0 * slope + row * flow_all[half, 1:2, :] - finals[half, 1:2, :]
            grad = (expo[index] * scale * (iota[...] * slope + rest)).astype(BF16)
            grads[index] = grad
            f_part[half] += matmul(k_all[origin], grad, ((0,), (0,)))
            return 0

        lax.fori_loop(0, n_z, step, 0)
        f_out[half] = f_part[half].astype(BF16)

    f_copies = []

    def send_half(half, dx):
        for i, (ox, dt) in enumerate(team):
            if ox == dx:
                _, t, where = mate_at(ox, dt)
                f_copies.append(
                    remote(
                        rows_of(f_out.at[half], t), f_in.at[slot], f_send.at[i],
                        f_recv.at[slot], where,
                    )
                )
                f_copies[-1].start()

    feat_half(other)
    send_half(other, 1)
    feat_half(xx)
    send_half(xx, 0)

    def target_terms(origin):
        return matmul(grads[origin], q_all[0], ((1,), (0,))) + matmul(
            grads[n_z + origin], q_all[1], ((1,), (0,))
        )

    def g_copy(z):
        return remote(
            g_out.at[z], g_in.at[zz], g_send.at[z], g_recv.at[zz], {"pb": z * 2 + xx}
        )

    def g_step(z):
        g_out[z] = target_terms(z).astype(BF16)
        g_copy(z).start()

    near(g_step)
    g2_ref[...] = target_terms(zz)

    total_f = f_part[xx, pl.ds(pl.multiple_of(grp * part, part), part), :]
    for i, (dx, dt) in enumerate(team):
        frm = source_at(dx, dt)
        remote(
            f_in.at[frm], f_in.at[frm], f_send.at[i], f_recv.at[frm], mate_at(dx, dt)[2]
        ).wait_recv()
        total_f = total_f + f_in[frm].astype(F32)
    feat_ref[pl.ds(pl.multiple_of(grp * part, part), part), :] = total_f.astype(BF16)
    a_copies = []
    for d in range(1, n_ta):
        to = lax.rem(grp + d, n_ta)
        a_copies.append(
            remote(
                rows_of(feat_ref, grp), rows_of(feat_ref, grp), a_send.at[d], a_recv.at[grp],
                {"ta": to},
            )
        )
        a_copies[-1].start()
    for d in range(1, n_ta):
        frm = lax.rem(grp + n_ta - d, n_ta)
        remote(
            rows_of(feat_ref, frm), rows_of(feat_ref, frm), a_send.at[d], a_recv.at[frm],
            {"ta": frm},
        ).wait_recv()

    feat = feat_ref[...]
    width = 3 * cin
    for a in range(3):
        gw_part[a * width : (a + 1) * width, :] = matmul(
            in_sh[:, a * cols : (a + rows) * cols], feat, ((1,), (1,))
        )
    gw_send[...] = gw_part[...].astype(BF16)

    def w_copy(index):
        return remote(
            gw_send.at[pl.ds(gw_start(index), gw_rows), :], gw_in.at[me],
            w_send.at[index], w_recv.at[me], {"pb": own_first + index},
        )

    def to_owners(fn):
        def step(index, _):
            @pl.when(index != own)
            def _():
                fn(index)

            return 0

        lax.fori_loop(0, n_own, step, 0)

    to_owners(lambda index: w_copy(index).start())

    spread = matmul(w_ref[...], feat, ((1,), (0,)))
    outs = [None] * (rows + 2)
    for r in range(rows):
        for a in range(3):
            term = None
            for b in range(3):
                first = (a * 3 + b) * cin
                piece = moved(
                    spread[first : first + cin, r * cols : (r + 1) * cols], b - 1
                )
                term = piece if term is None else term + piece
            place = r + a
            outs[place] = term if outs[place] is None else outs[place] + term
    edge_out[0] = outs[rows + 1].astype(BF16)
    edge_out[1] = outs[0].astype(BF16)
    e_up = remote(edge_out.at[0], edge_in.at[0], e_send.at[0], e_recv.at[0], up)
    e_down = remote(edge_out.at[1], edge_in.at[1], e_send.at[1], e_recv.at[1], down)
    e_up.start()
    e_down.start()
    for y in range(rows):
        gi_ref[y] = outs[y + 1]

    def v_copy(d):
        return remote(
            gw_sum, gw_all.at[own], v_send.at[d], v_recv.at[own],
            {"pb": lax.rem(me + d, n_pb)},
        )

    @pl.when(is_own)
    def _():
        def add(d, total):
            frm = lax.rem(me + n_pb - d, n_pb)
            remote(
                gw_in.at[frm], gw_in.at[frm], w_send.at[0], w_recv.at[frm], {"pb": frm}
            ).wait_recv()
            return total + gw_in[frm].astype(F32)

        total = lax.fori_loop(1, n_pb, add, gw_part[pl.ds(gw_start(own), gw_rows), :])
        gw_sum[...] = total.astype(BF16)

        def give(d, _):
            v_copy(d).start()
            return 0

        lax.fori_loop(1, n_pb, give, 0)
        gw_all[own] = gw_sum[...]

    def g_add(z):
        remote(
            g_in.at[z], g_in.at[z], g_send.at[z], g_recv.at[z], {"pb": z * 2 + xx}
        ).wait_recv()
        g2_ref[...] += g_in[z].astype(F32)

    near(g_add)

    e_up.wait_recv()
    e_down.wait_recv()
    gi_ref[0] += edge_in[0].astype(F32) * jnp.where(me == 0, 0.0, 1.0)
    gi_ref[rows - 1] += edge_in[1].astype(F32) * jnp.where(me == n_pb - 1, 0.0, 1.0)

    def v_wait(index):
        remote(
            gw_all.at[index], gw_all.at[index], v_send.at[0], v_recv.at[index],
            {"pb": own_first + index},
        ).wait_recv()

    to_owners(v_wait)

    def write(index, _):
        gw_ref[pl.ds(gw_start(index), gw_rows), :] = gw_all[index].astype(F32)
        return 0

    lax.fori_loop(0, n_own, write, 0)

    for copy in (
        q_copy, flow_copy, h_up, h_down, e_up, e_down, *stat_copies, *f_copies, *a_copies
    ):
        copy.wait_send()

    def gone(z):
        k_copy(z).wait_send()
        g_copy(z).wait_send()

    near(gone)

    to_owners(lambda index: w_copy(index).wait_send())

    @pl.when(is_own)
    def _():
        def drain(d, _):
            v_copy(d).wait_send()
            return 0

        lax.fori_loop(1, n_pb, drain, 0)


def place(g2_in, gi_in, gw_in, g2_ref, gi_ref, gw_ref, sem):
    copies = [
        pltpu.make_async_copy(src, dst, sem.at[i])
        for i, (src, dst) in enumerate(
            ((g2_in, g2_ref), (gi_in, gi_ref), (gw_in, gw_ref))
        )
    ]
    for copy in copies:
        copy.start()
    for copy in copies:
        copy.wait()


def per_device(n_pb, n_ta, feat_one, feat_two, cot_flow, enc_input, enc_weight):
    rows, cols, chan = feat_one.shape
    n_q = rows * cols
    tgt = feat_two.shape[1]
    cin = enc_input.shape[1]
    taps = 9 * cin
    assert n_pb % 4 == 0 and FRAME_COLS % tgt == 0 and taps % 16 == 0
    gw_rows = 16 * pl.cdiv(taps // 16, n_pb // 2)
    vmem = pl.BlockSpec(memory_space=pltpu.VMEM)
    dma = pltpu.SemaphoreType.DMA
    n_z = n_pb // 2
    shapes = ((tgt, chan), (rows, cin, cols), (taps, chan))
    outs = pl.pallas_call(
        functools.partial(kernel, n_pb, n_ta, rows, cols, gw_rows),
        out_shape=tuple(pltpu.VMEM(shape, F32) for shape in shapes),
        in_specs=[pl.BlockSpec(memory_space=pl.ANY)] * 5,
        out_specs=(vmem,) * 3,
        scratch_shapes=[
            pltpu.VMEM((2, rows, cols), F32),
            pltpu.VMEM((rows, cin, cols), BF16),
            pltpu.VMEM((taps, chan), BF16),
            dma((5,)),
            pltpu.VMEM((2, n_q, chan), BF16),
            pltpu.VMEM((2, rows, cols), F32),
            pltpu.VMEM((2, 8, n_q), F32),
            pltpu.VMEM((n_z, tgt, chan), BF16),
            pltpu.VMEM((n_pb, tgt, n_q), F32),
            pltpu.VMEM((n_pb, tgt, n_q), BF16),
            pltpu.VMEM((tgt, n_q), F32),
            pltpu.VMEM((n_pb, 1, n_q), F32),
            pltpu.VMEM((n_pb, 1, n_q), F32),
            pltpu.VMEM((n_pb, 1, n_q), F32),
            pltpu.VMEM((8, n_q), F32),
            pltpu.VMEM((2 * n_ta, 8, n_q), F32),
            pltpu.VMEM((2, 8, n_q), F32),
            pltpu.VMEM((n_z, tgt, chan), BF16),
            pltpu.VMEM((n_z, tgt, chan), BF16),
            pltpu.VMEM((2, chan, n_q), F32),
            pltpu.VMEM((2, chan, n_q), BF16),
            pltpu.VMEM((2 * n_ta, chan // n_ta, n_q), BF16),
            pltpu.VMEM((chan, n_q), BF16),
            pltpu.VMEM((2, cin, cols), BF16),
            pltpu.VMEM((3 * cin, (rows + 2) * cols), BF16),
            pltpu.VMEM((2, cin, cols), BF16),
            pltpu.VMEM((2, cin, cols), BF16),
            pltpu.VMEM((taps, chan), F32),
            pltpu.VMEM((taps, chan), BF16),
            pltpu.VMEM((n_pb, gw_rows, chan), BF16),
            pltpu.VMEM((gw_rows, chan), BF16),
            pltpu.VMEM((n_pb // 2, gw_rows, chan), BF16),
            dma((2,)), dma((2,)),
            dma((n_z,)), dma((n_z,)),
            dma((2 * n_ta,)), dma((2 * n_ta,)),
            dma((n_z,)), dma((n_z,)),
            dma((2 * n_ta,)), dma((2 * n_ta,)),
            dma((n_ta,)), dma((n_ta,)),
            dma((2,)), dma((2,)),
            dma((2,)), dma((2,)),
            dma((n_pb // 2,)), dma((n_pb,)),
            dma((n_pb,)), dma((n_pb // 2,)),
        ],
        compiler_params=pltpu.CompilerParams(collective_id=0, has_side_effects=True),
        name="matching",
    )(
        feat_one.reshape(n_q, chan),
        feat_two[0],
        cot_flow,
        enc_input,
        enc_weight.reshape(taps, chan),
    )
    outs = pl.pallas_call(
        place,
        out_shape=tuple(jax.ShapeDtypeStruct(shape, F32) for shape in shapes),
        in_specs=[vmem] * 3,
        out_specs=(pl.BlockSpec(memory_space=pl.ANY),) * 3,
        scratch_shapes=[dma((3,))],
        name="place",
    )(*(pltpu.with_memory_space_constraint(out, pltpu.VMEM) for out in outs))
    return (
        outs[0][None],
        outs[1],
        outs[2].reshape(3, 3, cin, chan),
    )


def solution(mesh):
    in_specs = (
        P("pb", None, None),
        P("ta", "pb", None),
        P(None, "pb", None),
        P("pb", "ta", None),
        P(None, None, "ta", None),
    )
    out_specs = (P("ta", "pb", None), P("pb", "ta", None), P(None, None, "ta", None))
    body = functools.partial(per_device, mesh.shape["pb"], mesh.shape["ta"])
    return jax.shard_map(
        body, mesh=mesh, in_specs=in_specs, out_specs=out_specs, check_vma=False
    )
```
